32 devices in a mesh: section: 2 (over x), dp: 4 (over y, core), expert: 4 (over z).
Axes of the slice: x: 2, y: 2, z: 4, core: 2. Of those that a mesh axis runs over, the one named last changes fastest.
Arguments:
- tokens: bfloat16 [2, 2048, 2560], P('section', ('dp', 'expert')), may hold values from -6 to 6
- cotangent: bfloat16 [2, 2048, 2560], P('section', ('dp', 'expert')), may hold values from -3 to 3
- routes: int32 [2, 2048, 6], P('section', ('dp', 'expert')), may hold values from 0 to 159, as said below
- gates: float32 [2, 2048, 6], P('section', ('dp', 'expert')), may hold values from 0.2 to 1
- gate_up: bfloat16 [2, 4, 2, 1024, 2560], P('section', 'expert', None, 'dp'), may hold values from -0.125 to 0.125
- down: bfloat16 [2, 4, 1024, 2560], P('section', 'expert', 'dp'), may hold values from -0.1875 to 0.1875
Outputs:
- handed_on: bfloat16 [2, 2048, 2560], P('section', ('dp', 'expert'))
- handed_back: bfloat16 [2, 2048, 2560], P('section', ('dp', 'expert'))
- grad_gate_up: bfloat16 [2, 4, 2, 1024, 2560], P('section', 'expert', None, 'dp')
- grad_down: bfloat16 [2, 4, 1024, 2560], P('section', 'expert', 'dp')
The draws below stay inside these ranges and needn't reach their ends.
Inputs may be any that keep to these rules, and one draw needn't show every extreme that they name: `routes`: A token's 6 ids are distinct and at most one of them is below 4. In each device's block of 128 tokens no id below 4 is named by more than 32 tokens.
All inputs are finite; a program needn't handle non-finite values.
Results may differ from the reference program's by a relative error of at most 0.0065.
Values may be sent and summed in bfloat16 or wider, within the bound.
No kernel may reach another device: no remote copies, remote signals or barrier semaphores. Data moves between devices by JAX's collectives and lax.ppermute only.
A program may use at most 64 MiB of HBM per device.

```python
import jax
import jax.numpy as jnp
from jax import lax

D = 2560
H = 1024
EXPERTS_ALL = 160
TOP = 6
TOK_DEV = 128
SECTIONS = 2
WIN = 4
CAP = 32
ROWS = 2048
N_DP = 4
N_EXPERT = 4


def draw_routes(key, part):
    keys = jax.random.split(key, 5)
    labels = jnp.arange(WIN, dtype=jnp.int32)
    favoured = jax.random.randint(keys[0], (SECTIONS, N_DP, 1, 1), 0, WIN)
    counts = jax.random.randint(keys[1], (SECTIONS, N_DP, N_EXPERT, WIN), 0, CAP + 1)
    counts = jnp.where(labels == favoured, CAP, counts)
    starts = jnp.cumsum(counts, -1) - counts
    places = jnp.arange(TOK_DEV, dtype=jnp.int32)[:, None]
    inside = (places >= starts[..., None, :]) & (places < (starts + counts)[..., None, :])
    covered = jnp.any(inside, -1)
    owner = jnp.sum(jnp.where(inside, labels, 0), -1)
    scores = jax.random.randint(keys[2], (SECTIONS, N_DP, N_EXPERT, TOK_DEV), 0, 1 << 20) * TOK_DEV
    scores = scores + jnp.arange(TOK_DEV, dtype=jnp.int32)
    ordering = jnp.argsort(scores, -1)
    position = jnp.argsort(ordering, -1)
    row_owner = jnp.take_along_axis(owner, position, -1)
    row_covered = jnp.take_along_axis(covered, position, -1)
    outside = EXPERTS_ALL - WIN
    fills = jax.random.randint(keys[3], (SECTIONS, N_DP, N_EXPERT, TOK_DEV, outside), 0, 1 << 20) * 256
    fills = fills + jnp.arange(outside, dtype=jnp.int32)
    unused, picks = lax.top_k(fills, TOP)
    picks = picks.astype(jnp.int32) + WIN
    leading = jnp.where(row_covered, row_owner, picks[..., 0])
    chosen = jnp.concatenate([leading[..., None], picks[..., 1:]], -1)
    mixing = jax.random.randint(keys[4], (SECTIONS, N_DP, N_EXPERT, TOK_DEV, TOP), 0, 1 << 20) * 8
    mixing = mixing + jnp.arange(TOP, dtype=jnp.int32)
    shuffle = jnp.argsort(mixing, -1)
    routes = jnp.take_along_axis(chosen, shuffle, -1)
    return routes.reshape(SECTIONS, N_DP * N_EXPERT * TOK_DEV, TOP).astype(jnp.int32)


def level_of(stream_key, dims, cuts, least, top_value):
    gain, own = 1.0, jax.random.fold_in(stream_key, 6)
    for axis_at, shards_of in cuts:
        draws = jnp.exp(jax.random.uniform(jax.random.fold_in(own, axis_at), (shards_of,), jnp.float32, least / len(cuts), top_value / len(cuts)))
        gain = gain * jnp.repeat(draws, dims[axis_at] // shards_of).reshape([-1 if axis == axis_at else 1 for axis in range(len(dims))])
    return gain


def normal_values(rng, extent, width, limit, cuts=(), held_as=jnp.bfloat16):
    entries = width * jax.random.normal(rng, extent, jnp.float32)
    if cuts:
        entries = entries * level_of(rng, extent, cuts, -0.22, 0.18)
    return jnp.clip(entries, -limit, limit).astype(held_as)


def setup_inputs(seed: int = 0) -> dict:
    arg_keys = jax.random.split(jax.random.key(seed), 7)
    return {
        "tokens": normal_values(arg_keys[0], (SECTIONS, ROWS, D), 1.0, 6.0, ((0, 2), (1, 16))),
        "cotangent": normal_values(arg_keys[1], (SECTIONS, ROWS, D), 0.5, 3.0, ((0, 2), (1, 16))),
        "routes": draw_routes(jax.random.fold_in(arg_keys[6], 71), 0),
        "gates": jnp.clip(0.2 + 0.8 * jax.random.uniform(arg_keys[3], (SECTIONS, ROWS, TOP), jnp.float32) ** level_of(arg_keys[3], (SECTIONS, ROWS, TOP), ((0, 2), (1, 16)), -0.2, 0.2), 0.2, 1.0),
        "gate_up": normal_values(arg_keys[4], (SECTIONS, WIN, 2, H, D), D ** -0.5, 0.125, ((0, 2), (1, 4), (3, 4))),
        "down": normal_values(arg_keys[5], (SECTIONS, WIN, H, D), H ** -0.5, 0.1875, ((0, 2), (1, 4), (2, 4))),
    }


def expert_pass(operands):
    slot_rows, slot_grads, gate_up, down = operands
    quarter = H // N_DP
    row_count = slot_rows.shape[0]
    pre_gate = jnp.dot(slot_rows, gate_up[0].T, preferred_element_type=jnp.float32)
    pre_up = jnp.dot(slot_rows, gate_up[1].T, preferred_element_type=jnp.float32)
    sigmoid_gate = jax.nn.sigmoid(pre_gate)
    activated = pre_gate * sigmoid_gate
    hidden = (activated * pre_up).astype(jnp.bfloat16)
    hidden_split = hidden.astype(jnp.float32).reshape(row_count, N_DP, quarter)
    down_split = down.astype(jnp.float32).reshape(N_DP, quarter, D)
    parts = jnp.einsum("rqh,qhd->qrd", hidden_split, down_split)
    parts = lax.optimization_barrier(parts.astype(jnp.bfloat16))
    expert_out = jnp.sum(parts.astype(jnp.float32), 0).astype(jnp.bfloat16)
    hidden_grad = jnp.dot(slot_grads, down.T, preferred_element_type=jnp.float32)
    grad_down = jnp.dot(hidden.T, slot_grads, preferred_element_type=jnp.float32).astype(jnp.bfloat16)
    gate_slope = sigmoid_gate * (1.0 + pre_gate * (1.0 - sigmoid_gate))
    gate_grad = (hidden_grad * pre_up * gate_slope).astype(jnp.bfloat16)
    up_grad = (hidden_grad * activated).astype(jnp.bfloat16)
    grad_gate = jnp.dot(gate_grad.T, slot_rows, preferred_element_type=jnp.float32).astype(jnp.bfloat16)
    grad_up = jnp.dot(up_grad.T, slot_rows, preferred_element_type=jnp.float32).astype(jnp.bfloat16)
    weights_split = gate_up.astype(jnp.float32).reshape(2, N_DP, quarter, D)
    gate_split = gate_grad.astype(jnp.float32).reshape(row_count, N_DP, quarter)
    up_split = up_grad.astype(jnp.float32).reshape(row_count, N_DP, quarter)
    input_parts = jnp.einsum("rqh,qhd->qrd", gate_split, weights_split[0])
    input_parts = input_parts + jnp.einsum("rqh,qhd->qrd", up_split, weights_split[1])
    input_parts = lax.optimization_barrier(input_parts.astype(jnp.bfloat16))
    slot_input = jnp.sum(input_parts.astype(jnp.float32), 0).astype(jnp.bfloat16)
    return expert_out, slot_input, jnp.stack([grad_gate, grad_up]), grad_down


def section_pass(operands):
    tokens, cotangent, routes, gates, gate_up, down = operands
    blocks = N_DP * N_EXPERT
    capacity = TOK_DEV // N_EXPERT
    section_rows = tokens.shape[0]
    block_routes = routes.reshape(blocks, TOK_DEV, TOP)
    block_gates = gates.reshape(blocks, TOK_DEV, TOP)
    in_window = block_routes < N_EXPERT
    expert_of = jnp.sum(jnp.where(in_window, block_routes, 0), -1)
    present = jnp.any(in_window, -1)
    weight = jnp.sum(jnp.where(in_window, block_gates, 0.0), -1)
    member = ((expert_of[..., None] == jnp.arange(N_EXPERT)) & present[..., None]).astype(jnp.float32)
    before = jnp.cumsum(member, 1) - member
    slot_index = jnp.sum(before * member, -1)
    slot_values = jnp.arange(capacity).astype(jnp.float32)
    select = jnp.swapaxes(member, 1, 2)[:, :, None, :] * (slot_index[:, None, None, :] == slot_values[None, None, :, None])
    block_rows = tokens.astype(jnp.float32).reshape(blocks, TOK_DEV, D)
    slot_rows = jnp.einsum("bect,btd->ebcd", select, block_rows).astype(jnp.bfloat16)
    slot_rows = slot_rows.reshape(N_EXPERT, blocks * capacity, D)
    scaled = (cotangent.astype(jnp.float32).reshape(blocks, TOK_DEV, D) * weight[..., None]).astype(jnp.bfloat16)
    slot_grads = jnp.einsum("bect,btd->ebcd", select, scaled.astype(jnp.float32)).astype(jnp.bfloat16)
    slot_grads = slot_grads.reshape(N_EXPERT, blocks * capacity, D)
    expert_out, slot_input, grad_gate_up, grad_down = lax.map(expert_pass, (slot_rows, slot_grads, gate_up, down))
    expert_out = expert_out.astype(jnp.float32).reshape(N_EXPERT, blocks, capacity, D)
    mixture = jnp.einsum("bect,ebcd->btd", select, expert_out) * weight[..., None]
    slot_input = slot_input.astype(jnp.float32).reshape(N_EXPERT, blocks, capacity, D)
    input_grad = jnp.einsum("bect,ebcd->btd", select, slot_input).astype(jnp.bfloat16)
    mixture = mixture.astype(jnp.bfloat16).reshape(section_rows, D)
    return mixture, input_grad.reshape(section_rows, D), grad_gate_up, grad_down


def reference(tokens, cotangent, routes, gates, gate_up, down):
    mixture, input_grad, grad_gate_up, grad_down = lax.map(section_pass, (tokens, cotangent, routes, gates, gate_up, down))
    handed_on = jnp.concatenate([jnp.zeros_like(mixture[:1]), mixture[:-1]], 0)
    handed_back = jnp.concatenate([input_grad[1:], jnp.zeros_like(input_grad[:1])], 0)
    return handed_on, handed_back, grad_gate_up, grad_down
```

```python
import functools

import jax
import jax.numpy as jnp
from jax import lax
from jax.experimental import pallas as pl
from jax.experimental.pallas import tpu as pltpu
from jax.sharding import PartitionSpec as P


AXES = ("section", "dp", "expert")
LAST = (((1,), (1,)), ((), ()))
FIRST = (((0,), (0,)), ((), ()))
PLAIN = (((1,), (0,)), ((), ()))
IN_VMEM = pl.BlockSpec(memory_space=pltpu.VMEM)
IN_SMEM = pl.BlockSpec(memory_space=pltpu.SMEM)


def moved(value, target):
    sizes = [lax.axis_size(axis) for axis in AXES]
    pairs = []
    for s in range(sizes[0]):
        for d in range(sizes[1]):
            for e in range(sizes[2]):
                to = target(s, d, e)
                if to is not None:
                    source = (s * sizes[1] + d) * sizes[2] + e
                    pairs.append((source, (to[0] * sizes[1] + to[1]) * sizes[2] + to[2]))
    return lax.ppermute(value, AXES, pairs)


def dot(a, b, dims=PLAIN):
    return lax.dot_general(a, b, dims, preferred_element_type=jnp.float32)


def call(body, outs, operands, name, mib, scratch=(), smem=1):
    return pl.pallas_call(
        body,
        out_shape=outs,
        in_specs=[IN_SMEM] * smem + [IN_VMEM] * (len(operands) - smem),
        out_specs=[IN_VMEM] * len(outs),
        scratch_shapes=scratch,
        compiler_params=pltpu.CompilerParams(vmem_limit_bytes=mib << 20),
        name=name,
    )(*operands)


def column_of(row):
    n = row.shape[1]
    diagonal = lax.broadcasted_iota(jnp.int32, (n, n), 0) == lax.broadcasted_iota(jnp.int32, (n, n), 1)
    return jnp.sum(jnp.where(diagonal, row, 0.0), 1, keepdims=True)


def pack_body(window, lanes, where_ref, routes, gates, tokens, cotangent, *outs):
    section, column = where_ref[0], where_ref[1]
    packed, info = outs[:window], outs[window]
    rows_here = tokens.shape[0]
    capacity = rows_here // window
    in_window = routes[...] < window
    expert_of = jnp.sum(jnp.where(in_window, routes[...], 0), 0, keepdims=True)
    present = jnp.sum(jnp.where(in_window, 1, 0), 0, keepdims=True) > 0
    weight = jnp.sum(jnp.where(in_window, gates[...], 0.0), 0, keepdims=True)
    distance = expert_of - column
    distance = jnp.where(distance < 0, distance + window, distance)
    code = jnp.where(present, distance, -1).astype(jnp.float32)
    square = (rows_here, rows_here)
    down_index = lax.broadcasted_iota(jnp.int32, square, 0)
    along_index = lax.broadcasted_iota(jnp.int32, square, 1)
    earlier = (column_of(code) == code) & (down_index < along_index)
    slot = jnp.sum(jnp.where(earlier, 1.0, 0.0), 0, keepdims=True)
    place = jnp.where(present, code * capacity + slot, -1.0)
    select = jnp.where(down_index.astype(jnp.float32) == place, 1.0, 0.0).astype(jnp.bfloat16)
    scaled = (cotangent[...].astype(jnp.float32) * column_of(weight)).astype(jnp.bfloat16)
    slot_rows = dot(select, tokens[...]).astype(jnp.bfloat16)
    slot_grads = dot(select, scaled).astype(jnp.bfloat16)
    for k in range(window):
        packed[k][0] = slot_rows[k * capacity : (k + 1) * capacity]
        packed[k][1] = slot_grads[k * capacity : (k + 1) * capacity]
    for i, (kind, _) in enumerate(lanes):
        ones = jnp.ones_like(weight)
        scale = {"up": weight, "down": ones, "swap": jnp.where(section == 0, weight, ones)}[kind]
        info[i, 0:1] = place
        info[i, 1:2] = scale


def chunk_body(lanes, groups, where_ref, *refs):
    section = where_ref[0]
    pieces, refs = refs[:groups], refs[groups:]
    (gate_up_here, down_here, gate_up_pair, down_pair), refs = refs[:4], refs[4:]
    outs, (kept, sent) = refs[:-2], refs[-2:]
    rows = jnp.concatenate([piece[0] for piece in pieces])
    grads = jnp.concatenate([piece[1] for piece in pieces])
    capacity, units = pieces[0].shape[1], down_here.shape[0]
    for gate_up, down, hidden_out in ((gate_up_here, down_here, kept), (gate_up_pair, down_pair, sent)):
        pre_gate = dot(rows, gate_up[0], LAST)
        pre_up = dot(rows, gate_up[1], LAST)
        hidden_grad = dot(grads, down[...], LAST)
        sigmoid = jax.nn.sigmoid(pre_gate)
        activated = pre_gate * sigmoid
        slope = sigmoid * (1.0 + pre_gate * (1.0 - sigmoid))
        hidden_out[:, :units] = (activated * pre_up).astype(jnp.bfloat16)
        hidden_out[:, units : 2 * units] = (hidden_grad * pre_up * slope).astype(jnp.bfloat16)
        hidden_out[:, 2 * units :] = (hidden_grad * activated).astype(jnp.bfloat16)

    def output_rows():
        return dot(kept[:, :units], down_here[...]) + dot(sent[:, :units], down_pair[...])

    def input_rows():
        total = None
        for gate_up, hidden in ((gate_up_here, kept), (gate_up_pair, sent)):
            for i in range(2):
                term = dot(hidden[:, (i + 1) * units : (i + 2) * units], gate_up[i])
                total = term if total is None else total + term
        return total

    def store(i, total):
        for j in range(groups):
            out = outs[i * groups + j]
            out[...] = total[j * capacity : (j + 1) * capacity].astype(out.dtype)

    for i, (kind, _) in enumerate(lanes):
        if kind == "up":
            store(i, output_rows())
        elif kind == "down":
            store(i, input_rows())
        else:

            @pl.when(section == 0)
            def _():
                store(i, output_rows())

            @pl.when(section != 0)
            def _():
                store(i, input_rows())


def weights_body(which, columns, *refs):
    hidden_refs, piece_refs, out, hidden_all, piece_all = refs
    at = 0
    for ref in hidden_refs:
        hidden_all[at : at + ref.shape[0]] = ref[...]
        at += ref.shape[0]
    at = 0
    for ref in piece_refs:
        piece_all[at : at + ref.shape[1]] = ref[which]
        at += ref.shape[1]
    units = hidden_all.shape[1] // 3
    for i, c in enumerate(columns):
        value = dot(hidden_all[:, c * units : (c + 1) * units], piece_all[...], FIRST)
        out[i] = value.astype(out.dtype)


def final_body(mode, window, where_ref, info, *refs):
    section = where_ref[0]
    rows = jnp.concatenate([ref[...] for ref in refs[:window]])
    outs = refs[window:]
    place, scale = info[0:1], info[1:2]
    size = (rows.shape[0], place.shape[1])
    pick = jnp.where(lax.broadcasted_iota(jnp.int32, size, 0).astype(jnp.float32) == place, 1.0, 0.0)
    value = dot(pick.astype(jnp.bfloat16), rows, FIRST) * column_of(scale)
    value = value.astype(jnp.bfloat16)
    zero = jnp.zeros_like(value)
    for out, (lowest, highest) in zip(outs, mode):
        keep = (section >= lowest) & (section <= highest)
        out[...] = jnp.where(keep, value, zero)


def shards(tokens, cotangent, routes, gates, gate_up, down):
    sections, copies, window = (lax.axis_size(axis) for axis in AXES)
    groups = copies // 2
    rows_here, width = tokens.shape[1:]
    capacity = rows_here // window
    position = jnp.stack([lax.axis_index("section"), lax.axis_index("expert")]).astype(jnp.int32)

    def pair_of(s, d, e):
        return s, d ^ 1, e

    def group_shift(step):
        return lambda s, d, e: (s, (d // 2 + step) % groups * 2 + d % 2, e)

    def column_shift(step):
        return lambda s, d, e: (s, d, (e + step) % window)

    def owner_shift(up, step):
        def target(s, d, e):
            to = (s + up) % sections if sections == 2 else s + up
            return (to, d, (e + step) % window) if 0 <= to < sections else None

        return target

    lanes = (("swap", 1),) if sections == 2 else (("up", 1), ("down", -1))
    bf16 = functools.partial(jax.ShapeDtypeStruct, dtype=jnp.bfloat16)
    f32 = functools.partial(jax.ShapeDtypeStruct, dtype=jnp.float32)

    gate_up_here, down_here = gate_up[0, 0], down[0, 0]
    gate_up_pair = moved(gate_up_here, pair_of)
    down_pair = moved(down_here, pair_of)
    weights = (gate_up_here, down_here, gate_up_pair, down_pair)
    weights = tuple(pltpu.with_memory_space_constraint(w, pltpu.VMEM) for w in weights)

    *packed, info = call(
        functools.partial(pack_body, window, lanes),
        [bf16((2, capacity, width))] * window + [f32((len(lanes), 2, rows_here))],
        (position, routes[0].T, gates[0].T, tokens[0], cotangent[0]),
        "pack",
        12,
    )
    infos = [moved(info[i], owner_shift(up, 0)) for i, (_, up) in enumerate(lanes)]

    units = down_here.shape[0]
    chunk_rows = groups * capacity
    returned = [[None] * window for _ in lanes]
    kept_pieces, kept_hidden, sent_hidden = [], [], []
    for k in [0] + list(range(window - 1, 0, -1)):
        arrived = moved(packed[k], column_shift(k)) if k else packed[k]
        pieces = [arrived] + [moved(arrived, group_shift(j)) for j in range(1, groups)]
        part_shapes = [f32((capacity, width))] + [bf16((capacity, width))] * (groups - 1)
        *parts, kept, sent = call(
            functools.partial(chunk_body, lanes, groups),
            part_shapes * len(lanes) + [bf16((chunk_rows, 3 * units))] * 2,
            (position, *pieces, *weights),
            "chunk",
            12,
        )
        kept_pieces += pieces
        kept_hidden.append(kept)
        sent_hidden.append(sent)
        for i, (_, up) in enumerate(lanes):
            total = parts[i * groups]
            for j in range(1, groups):
                back = moved(parts[i * groups + j], group_shift(-j))
                total = total + back.astype(jnp.float32)
            returned[i][k] = moved(total.astype(jnp.bfloat16), owner_shift(up, -k))

    pieces = kept_pieces + [moved(piece, pair_of) for piece in kept_pieces]
    hidden = kept_hidden + [moved(value, pair_of) for value in sent_hidden]
    contracted = len(hidden) * chunk_rows

    def weights_call(which, columns, name):
        def body(*refs):
            n, m = len(hidden), len(pieces)
            weights_body(which, columns, refs[:n], refs[n : n + m], *refs[n + m :])

        return call(
            body,
            [bf16((len(columns), units, width))],
            (*hidden, *pieces),
            name,
            40,
            [
                pltpu.VMEM((contracted, 3 * units), jnp.bfloat16),
                pltpu.VMEM((contracted, width), jnp.bfloat16),
            ],
            smem=0,
        )[0]

    grad_down = weights_call(1, (0,), "grad_down")
    grad_gate_up = weights_call(0, (1, 2), "grad_gate_up")

    modes = {
        "swap": ((1, 1), (0, 0)),
        "up": ((1, sections - 1),),
        "down": ((0, sections - 2),),
    }
    results = []
    for i, (kind, _) in enumerate(lanes):
        results += call(
            functools.partial(final_body, modes[kind], window),
            [bf16((rows_here, width))] * len(modes[kind]),
            (position, infos[i], *returned[i]),
            "final",
            12,
        )
    return (results[0][None], results[1][None], grad_gate_up[None, None], grad_down[None])


def solution(mesh):
    tokens_spec = P("section", ("dp", "expert"), None)
    gate_up_spec = P("section", "expert", None, "dp", None)
    down_spec = P("section", "expert", "dp", None)
    return jax.shard_map(
        shards,
        mesh=mesh,
        in_specs=(tokens_spec,) * 4 + (gate_up_spec, down_spec),
        out_specs=(tokens_spec, tokens_spec, gate_up_spec, down_spec),
        check_vma=False,
    )
```

```python
import functools

import jax
import jax.numpy as jnp
from jax import lax
from jax.experimental import pallas as pl
from jax.experimental.pallas import tpu as pltpu
from jax.sharding import PartitionSpec as P


AXES = ("section", "dp", "expert")
LAST = (((1,), (1,)), ((), ()))
FIRST = (((0,), (0,)), ((), ()))
PLAIN = (((1,), (0,)), ((), ()))
IN_VMEM = pl.BlockSpec(memory_space=pltpu.VMEM)
IN_HBM = pl.BlockSpec(memory_space=pltpu.HBM)
IN_SMEM = pl.BlockSpec(memory_space=pltpu.SMEM)


def moved(value, target):
    sizes = [lax.axis_size(axis) for axis in AXES]
    pairs = []
    for s in range(sizes[0]):
        for d in range(sizes[1]):
            for e in range(sizes[2]):
                to = target(s, d, e)
                if to is not None:
                    source = (s * sizes[1] + d) * sizes[2] + e
                    pairs.append((source, (to[0] * sizes[1] + to[1]) * sizes[2] + to[2]))
    return lax.ppermute(value, AXES, pairs)


def in_hbm(value):
    return pltpu.with_memory_space_constraint(value, pltpu.HBM)


def dot(a, b, dims=PLAIN):
    return lax.dot_general(a, b, dims, preferred_element_type=jnp.float32)


def call(body, outs, operands, mib, scratch=(), smem=1):
    return pl.pallas_call(
        body,
        out_shape=outs,
        in_specs=[IN_SMEM] * smem + [IN_VMEM] * (len(operands) - smem),
        out_specs=[IN_VMEM] * len(outs),
        scratch_shapes=scratch,
        compiler_params=pltpu.CompilerParams(vmem_limit_bytes=mib << 20),
    )(*operands)


def column_of(row):
    n = row.shape[1]
    diagonal = lax.broadcasted_iota(jnp.int32, (n, n), 0) == lax.broadcasted_iota(jnp.int32, (n, n), 1)
    return jnp.sum(jnp.where(diagonal, row, 0.0), 1, keepdims=True)


def pack_body(window, units, lanes, where_ref, routes, gates, tokens, cotangent, *refs):
    section, column = where_ref[0], where_ref[1]
    packed, info, refs = refs[: len(units)], refs[len(units)], refs[len(units) + 1 :]
    tokens_here, cotangent_here, routes_here, gates_here, sems, small_sems = refs
    rows_here, width = tokens.shape
    capacity = rows_here // window
    blocks = 4 if width % 512 == 0 else 1
    step = width // blocks
    small = [
        pltpu.make_async_copy(far, near, small_sems.at[which])
        for which, (far, near) in enumerate(((routes, routes_here), (gates, gates_here)))
    ]
    for copy in small:
        copy.start()
    copies = []
    for which, (far, near) in enumerate(((tokens, tokens_here), (cotangent, cotangent_here))):
        for b in range(blocks):
            at = pl.ds(b * step, step)
            copies.append(pltpu.make_async_copy(far.at[:, at], near.at[:, at], sems.at[which, b]))
            copies[-1].start()
    for copy in small:
        copy.wait()
    expert_of = jnp.full((1, rows_here), -1, jnp.int32)
    weight = jnp.zeros((1, rows_here), jnp.float32)
    for i in range(routes.shape[0]):
        in_window = routes_here[i] < window
        expert_of = jnp.where(in_window, routes_here[i], expert_of)
        weight = jnp.where(in_window, gates_here[i], weight)
    present = expert_of >= 0
    distance = expert_of - column
    distance = jnp.where(distance < 0, distance + window, distance)
    code = jnp.where(present, distance, -1).astype(jnp.float32)
    square = (rows_here, rows_here)
    down_index = lax.broadcasted_iota(jnp.int32, square, 0)
    along_index = lax.broadcasted_iota(jnp.int32, square, 1)
    earlier = (column_of(code) == code) & (down_index < along_index)
    slot = jnp.sum(jnp.where(earlier, 1.0, 0.0), 0, keepdims=True)
    place = jnp.where(present, code * capacity + slot, -1.0)
    select = jnp.where(down_index.astype(jnp.float32) == place, 1.0, 0.0).astype(jnp.bfloat16)
    for i, (kind, _) in enumerate(lanes):
        ones = jnp.ones_like(weight)
        scale = {"up": weight, "down": ones, "swap": jnp.where(section == 0, weight, ones)}[kind]
        info[i, 0:1] = place
        info[i, 1:2] = scale
    scale_column = column_of(weight)
    for which in range(2):
        for b in range(blocks):
            at = slice(b * step, (b + 1) * step)
            copies[which * blocks + b].wait()
            if which:
                block = (cotangent_here[:, at].astype(jnp.float32) * scale_column).astype(jnp.bfloat16)
            else:
                block = tokens_here[:, at]
            slots = dot(select, block).astype(jnp.bfloat16)
            for out, (k, low, high) in zip(packed, units):
                out[which, :, at] = slots[k * capacity + low : k * capacity + high]


def fetch_body(blocks, gate_up, down, gate_up_out, down_out, sems):
    copies = []
    for which, (far, near) in enumerate(((gate_up.at[0], gate_up_out.at[0]), (gate_up.at[1], gate_up_out.at[1]), (down, down_out))):
        step = far.shape[0] // blocks
        for b in range(blocks):
            at = pl.ds(b * step, step)
            copies.append(pltpu.make_async_copy(far.at[at], near.at[at], sems.at[which, b]))
            copies[-1].start()
    for copy in copies:
        copy.wait()


def chunk_body(lanes, groups, merges, where_ref, *refs):
    section = where_ref[0]
    count = groups * sum(len(merge) for merge in merges)
    pieces, refs = refs[:count], refs[count:]
    (gate_up_here, down_here, gate_up_pair, down_pair), refs = refs[:4], refs[4:]
    outs, (kept, bundle) = refs[:-2], refs[-2:]
    units, width = down_here.shape
    bounds = [0]
    for piece in pieces:
        bounds.append(bounds[-1] + piece.shape[1])
        at = slice(bounds[-2], bounds[-1])
        bundle[at, :width] = piece[0]
        bundle[at, width : 2 * width] = piece[1]
    rows, grads = bundle[:, :width], bundle[:, width : 2 * width]
    sent = bundle.at[:, 2 * width :]
    for gate_up, down, hidden_out in ((gate_up_here, down_here, kept), (gate_up_pair, down_pair, sent)):
        pre_gate = dot(rows, gate_up[0], LAST)
        pre_up = dot(rows, gate_up[1], LAST)
        hidden_grad = dot(grads, down[...], LAST)
        sigmoid = jax.nn.sigmoid(pre_gate)
        activated = pre_gate * sigmoid
        slope = sigmoid * (1.0 + pre_gate * (1.0 - sigmoid))
        hidden_out[:, :units] = (activated * pre_up).astype(jnp.bfloat16)
        hidden_out[:, units : 2 * units] = (hidden_grad * pre_up * slope).astype(jnp.bfloat16)
        hidden_out[:, 2 * units :] = (hidden_grad * activated).astype(jnp.bfloat16)

    def output_rows():
        return dot(kept[:, :units], down_here[...]) + dot(sent[:, :units], down_pair[...])

    def input_rows():
        total = None
        for gate_up, hidden in ((gate_up_here, kept), (gate_up_pair, sent)):
            for i in range(2):
                term = dot(hidden[:, (i + 1) * units : (i + 2) * units], gate_up[i])
                total = term if total is None else total + term
        return total

    def store(i, total):
        for m, merge in enumerate(merges):
            for j in range(groups):
                out = outs[(i * len(merges) + m) * groups + j]
                at = 0
                for u in merge:
                    low, high = bounds[u * groups + j], bounds[u * groups + j + 1]
                    out[at : at + high - low] = total[low:high].astype(out.dtype)
                    at += high - low

    for i, (kind, _) in enumerate(lanes):
        if kind == "up":
            store(i, output_rows())
        elif kind == "down":
            store(i, input_rows())
        else:

            @pl.when(section == 0)
            def _():
                store(i, output_rows())

            @pl.when(section != 0)
            def _():
                store(i, input_rows())


def weights_body(which, columns, hidden_refs, piece_refs, bundles, out, hidden_all, piece_all):
    units, width = out.shape[1:]
    at = 0
    for ref in hidden_refs:
        hidden_all[at : at + ref.shape[0]] = ref[...]
        at += ref.shape[0]
    at = 0
    for ref in piece_refs:
        piece_all[at : at + ref.shape[1]] = ref[which]
        at += ref.shape[1]
    for ref in bundles:
        piece_all[at : at + ref.shape[0]] = ref[:, which * width : (which + 1) * width]
        hidden_all[at : at + ref.shape[0]] = ref[:, 2 * width :]
        at += ref.shape[0]
    for i, c in enumerate(columns):
        value = dot(hidden_all[:, c * units : (c + 1) * units], piece_all[...], FIRST)
        out[i] = value.astype(out.dtype)


def final_body(mode, returns, where_ref, info, *refs):
    section = where_ref[0]
    sorted_refs = [refs[r] for r in sorted(range(len(returns)), key=lambda r: returns[r])]
    rows = jnp.concatenate([ref[...] for ref in sorted_refs])
    outs = refs[len(returns) :]
    place, scale = info[0:1], info[1:2]
    size = (rows.shape[0], place.shape[1])
    pick = jnp.where(lax.broadcasted_iota(jnp.int32, size, 0).astype(jnp.float32) == place, 1.0, 0.0)
    value = dot(pick.astype(jnp.bfloat16), rows, FIRST) * column_of(scale)
    value = value.astype(jnp.bfloat16)
    zero = jnp.zeros_like(value)
    for out, (lowest, highest) in zip(outs, mode):
        keep = (section >= lowest) & (section <= highest)
        out[...] = jnp.where(keep, value, zero)


def plan(window, capacity):
    if window < 4:
        units = [(k, 0, capacity) for k in range(window)]
        return units, [[[k] for k in range(window)]]
    half = capacity // 2
    units = [(k, 0, capacity) for k in range(2)]
    for k in range(2, window):
        units += [(k, 0, half), (k, half, capacity)]
    pairs = [[[u, u + 1]] for u in range(2, len(units), 2)]
    return units, [[[0]], [[1]]] + pairs


def computed(tokens, cotangent, routes, gates, gate_up, down):
    sections, copies, window = (lax.axis_size(axis) for axis in AXES)
    groups = copies // 2
    rows_here, width = tokens.shape[1:]
    capacity = rows_here // window
    position = jnp.stack([lax.axis_index("section"), lax.axis_index("expert")]).astype(jnp.int32)

    def pair_of(s, d, e):
        return s, d ^ 1, e

    def group_shift(step):
        return lambda s, d, e: (s, (d // 2 + step) % groups * 2 + d % 2, e)

    def column_shift(step):
        return lambda s, d, e: (s, d, (e + step) % window)

    def owner_shift(up, step):
        def target(s, d, e):
            to = (s + up) % sections if sections == 2 else s + up
            return (to, d, (e + step) % window) if 0 <= to < sections else None

        return target

    lanes = (("swap", 1),) if sections == 2 else (("up", 1), ("down", -1))
    bf16 = functools.partial(jax.ShapeDtypeStruct, dtype=jnp.bfloat16)
    f32 = functools.partial(jax.ShapeDtypeStruct, dtype=jnp.float32)

    units, chunks = plan(window, capacity)
    step = width // 4 if width % 512 == 0 else width
    *packed, info = pl.pallas_call(
        functools.partial(pack_body, window, units, lanes),
        out_shape=[bf16((2, high - low, width)) for _, low, high in units] + [f32((len(lanes), 2, rows_here))],
        in_specs=[IN_SMEM] + [IN_HBM] * 4,
        out_specs=[IN_VMEM] * (len(units) + 1),
        scratch_shapes=[pltpu.VMEM((rows_here, width), jnp.bfloat16)] * 2
        + [pltpu.VMEM((routes.shape[2], 1, rows_here), dtype) for dtype in (routes.dtype, gates.dtype)]
        + [pltpu.SemaphoreType.DMA((2, width // step)), pltpu.SemaphoreType.DMA((2,))],
        compiler_params=pltpu.CompilerParams(vmem_limit_bytes=12 << 20),
        name="pack",
    )(
        position,
        in_hbm(jnp.transpose(routes, (2, 0, 1))),
        in_hbm(jnp.transpose(gates, (2, 0, 1))),
        in_hbm(tokens[0]),
        in_hbm(cotangent[0]),
    )
    infos = [moved(info[i], owner_shift(up, 0)) for i, (_, up) in enumerate(lanes)]

    gate_up_here, down_here = gate_up[0, 0], down[0, 0]
    gate_up_pair = moved(gate_up_here, pair_of)
    down_pair = moved(down_here, pair_of)
    hidden_units = down_here.shape[0]
    gate_up_here, down_here = pl.pallas_call(
        functools.partial(fetch_body, 2),
        out_shape=[bf16(gate_up_here.shape), bf16(down_here.shape)],
        in_specs=[IN_HBM] * 2,
        out_specs=[IN_VMEM] * 2,
        scratch_shapes=[pltpu.SemaphoreType.DMA((3, 2))],
        compiler_params=pltpu.CompilerParams(vmem_limit_bytes=12 << 20),
        name="fetch",
    )(in_hbm(gate_up_here), in_hbm(down_here))
    weights = (gate_up_here, down_here, gate_up_pair, down_pair)
    weights = tuple(pltpu.with_memory_space_constraint(w, pltpu.VMEM) for w in weights)

    arrived = [moved(packed[u], column_shift(k)) if k else packed[u] for u, (k, _, _) in enumerate(units)]
    returned = [[] for _ in lanes]
    returns = []
    kept_pieces, kept_hidden, bundles = [], [], []
    for chunk in chunks:
        pieces, part_shapes, merges = [], [], []
        for merge in chunk:
            merges.append([len(pieces) // groups + m for m in range(len(merge))])
            for u in merge:
                pieces += [moved(arrived[u], group_shift(j)) if j else arrived[u] for j in range(groups)]
            size = (sum(units[u][2] - units[u][1] for u in merge), width)
            part_shapes += [f32(size)] + [bf16(size)] * (groups - 1)
            returns.append(units[merge[0]])
        chunk_rows = sum(piece.shape[1] for piece in pieces)
        *parts, kept, bundle = call(
            functools.partial(chunk_body, lanes, groups, merges),
            part_shapes * len(lanes)
            + [bf16((chunk_rows, 3 * hidden_units)), bf16((chunk_rows, 2 * width + 3 * hidden_units))],
            (position, *pieces, *weights),
            16,
        )
        kept_pieces += pieces
        kept_hidden.append(kept)
        bundles.append(moved(bundle, pair_of))
        for i, (_, up) in enumerate(lanes):
            for m, merge in enumerate(chunk):
                at = (i * len(chunk) + m) * groups
                total = parts[at]
                for j in range(1, groups):
                    back = moved(parts[at + j], group_shift(-j))
                    total = total + back.astype(jnp.float32)
                returned[i].append(moved(total.astype(jnp.bfloat16), owner_shift(up, -units[merge[0]][0])))

    def weights_call(which, columns):
        operands = (*kept_hidden, *kept_pieces, *bundles)
        n, m = len(kept_hidden), len(kept_hidden) + len(kept_pieces)

        def body(*refs):
            at = len(operands)
            weights_body(which, columns, refs[:n], refs[n:m], refs[m:at], *refs[at:])

        contracted = 2 * sum(piece.shape[1] for piece in kept_pieces)
        return call(
            body,
            [bf16((len(columns), hidden_units, width))],
            operands,
            16,
            [
                pltpu.VMEM((contracted, 3 * hidden_units), jnp.bfloat16),
                pltpu.VMEM((contracted, width), jnp.bfloat16),
            ],
            smem=0,
        )[0]

    grad_down = weights_call(1, (0,))
    grad_gate_up = weights_call(0, (1, 2))

    modes = {
        "swap": ((1, 1), (0, 0)),
        "up": ((1, sections - 1),),
        "down": ((0, sections - 2),),
    }
    results = []
    for i, (kind, _) in enumerate(lanes):
        results += call(
            functools.partial(final_body, modes[kind], returns),
            [bf16((rows_here, width))] * len(modes[kind]),
            (position, infos[i], *returned[i]),
            12,
        )
    return (results[0][None], results[1][None], grad_gate_up[None, None], grad_down[None])


def solution(mesh):
    tokens_spec = P("section", ("dp", "expert"), None)
    gate_up_spec = P("section", "expert", None, "dp", None)
    down_spec = P("section", "expert", "dp", None)
    return jax.shard_map(
        computed,
        mesh=mesh,
        in_specs=(tokens_spec,) * 4 + (gate_up_spec, down_spec),
        out_specs=(tokens_spec, tokens_spec, gate_up_spec, down_spec),
        check_vma=False,
    )
```

```python
import functools

import jax
import jax.numpy as jnp
from jax import lax
from jax.experimental import pallas as pl
from jax.experimental.pallas import tpu as pltpu
from jax.sharding import PartitionSpec as P


AXES = ("section", "dp", "expert")
LAST = (((1,), (1,)), ((), ()))
FIRST = (((0,), (0,)), ((), ()))
PLAIN = (((1,), (0,)), ((), ()))
IN_VMEM = pl.BlockSpec(memory_space=pltpu.VMEM)
IN_HBM = pl.BlockSpec(memory_space=pltpu.HBM)
IN_SMEM = pl.BlockSpec(memory_space=pltpu.SMEM)


def moved(value, target):
    sizes = [lax.axis_size(axis) for axis in AXES]
    pairs = []
    for s in range(sizes[0]):
        for d in range(sizes[1]):
            for e in range(sizes[2]):
                to = target(s, d, e)
                if to is not None:
                    source = (s * sizes[1] + d) * sizes[2] + e
                    pairs.append((source, (to[0] * sizes[1] + to[1]) * sizes[2] + to[2]))
    return lax.ppermute(value, AXES, pairs)


def in_hbm(value):
    return pltpu.with_memory_space_constraint(value, pltpu.HBM)


def dot(a, b, dims=PLAIN):
    return lax.dot_general(a, b, dims, preferred_element_type=jnp.float32)


def call(body, outs, operands, mib, scratch=(), smem=1):
    return pl.pallas_call(
        body,
        out_shape=outs,
        in_specs=[IN_SMEM] * smem + [IN_VMEM] * (len(operands) - smem),
        out_specs=[IN_VMEM] * len(outs),
        scratch_shapes=scratch,
        compiler_params=pltpu.CompilerParams(vmem_limit_bytes=mib << 20),
    )(*operands)


def column_of(row):
    n = row.shape[1]
    diagonal = lax.broadcasted_iota(jnp.int32, (n, n), 0) == lax.broadcasted_iota(jnp.int32, (n, n), 1)
    return jnp.sum(jnp.where(diagonal, row, 0.0), 1, keepdims=True)


def pack_body(window, units, lanes, where_ref, routes, gates, tokens, cotangent, *refs):
    section, column = where_ref[0], where_ref[1]
    packed, info, refs = refs[: len(units)], refs[len(units)], refs[len(units) + 1 :]
    tokens_here, cotangent_here, routes_here, gates_here, sems, small_sems = refs
    rows_here, width = tokens.shape
    capacity = rows_here // window
    blocks = 4 if width % 512 == 0 else 1
    step = width // blocks
    small = [
        pltpu.make_async_copy(far, near, small_sems.at[which])
        for which, (far, near) in enumerate(((routes, routes_here), (gates, gates_here)))
    ]
    for copy in small:
        copy.start()
    copies = []
    for which, (far, near) in enumerate(((tokens, tokens_here), (cotangent, cotangent_here))):
        for b in range(blocks):
            at = pl.ds(b * step, step)
            copies.append(pltpu.make_async_copy(far.at[:, at], near.at[:, at], sems.at[which, b]))
            copies[-1].start()
    for copy in small:
        copy.wait()
    expert_of = jnp.full((1, rows_here), -1, jnp.int32)
    weight = jnp.zeros((1, rows_here), jnp.float32)
    for i in range(routes.shape[0]):
        in_window = routes_here[i] < window
        expert_of = jnp.where(in_window, routes_here[i], expert_of)
        weight = jnp.where(in_window, gates_here[i], weight)
    present = expert_of >= 0
    distance = expert_of - column
    distance = jnp.where(distance < 0, distance + window, distance)
    code = jnp.where(present, distance, -1).astype(jnp.float32)
    square = (rows_here, rows_here)
    down_index = lax.broadcasted_iota(jnp.int32, square, 0)
    along_index = lax.broadcasted_iota(jnp.int32, square, 1)
    earlier = (column_of(code) == code) & (down_index < along_index)
    slot = jnp.sum(jnp.where(earlier, 1.0, 0.0), 0, keepdims=True)
    place = jnp.where(present, code * capacity + slot, -1.0)
    select = jnp.where(down_index.astype(jnp.float32) == place, 1.0, 0.0).astype(jnp.bfloat16)
    for i, (kind, _) in enumerate(lanes):
        ones = jnp.ones_like(weight)
        scale = {"up": weight, "down": ones, "swap": jnp.where(section == 0, weight, ones)}[kind]
        info[i, 0:1] = place
        info[i, 1:2] = scale
    scale_column = column_of(weight)
    for which in range(2):
        for b in range(blocks):
            at = slice(b * step, (b + 1) * step)
            copies[which * blocks + b].wait()
            if which:
                block = (cotangent_here[:, at].astype(jnp.float32) * scale_column).astype(jnp.bfloat16)
            else:
                block = tokens_here[:, at]
            slots = dot(select, block).astype(jnp.bfloat16)
            for out, (k, low, high) in zip(packed, units):
                out[which, :, at] = slots[k * capacity + low : k * capacity + high]


def fetch_body(blocks, gate_up, down, gate_up_out, down_out, sems):
    copies = []
    for which, (far, near) in enumerate(((gate_up.at[0], gate_up_out.at[0]), (gate_up.at[1], gate_up_out.at[1]), (down, down_out))):
        step = far.shape[0] // blocks
        for b in range(blocks):
            at = pl.ds(b * step, step)
            copies.append(pltpu.make_async_copy(far.at[at], near.at[at], sems.at[which, b]))
            copies[-1].start()
    for copy in copies:
        copy.wait()


def chunk_body(lanes, groups, merges, where_ref, *refs):
    section = where_ref[0]
    count = groups * sum(len(merge) for merge in merges)
    pieces, refs = refs[:count], refs[count:]
    (gate_up_here, down_here, gate_up_pair, down_pair), refs = refs[:4], refs[4:]
    outs, (kept, bundle) = refs[:-2], refs[-2:]
    units, width = down_here.shape
    bounds = [0]
    for piece in pieces:
        bounds.append(bounds[-1] + piece.shape[1])
        at = slice(bounds[-2], bounds[-1])
        bundle[at, :width] = piece[0]
        bundle[at, width : 2 * width] = piece[1]
    rows, grads = bundle[:, :width], bundle[:, width : 2 * width]
    sent = bundle.at[:, 2 * width :]
    for gate_up, down, hidden_out in ((gate_up_here, down_here, kept), (gate_up_pair, down_pair, sent)):
        pre_gate = dot(gate_up[0], rows, LAST).T
        pre_up = dot(gate_up[1], rows, LAST).T
        hidden_grad = dot(down[...], grads, LAST).T
        sigmoid = jax.nn.sigmoid(pre_gate)
        activated = pre_gate * sigmoid
        slope = sigmoid * (1.0 + pre_gate * (1.0 - sigmoid))
        hidden_out[:, :units] = (activated * pre_up).astype(jnp.bfloat16)
        hidden_out[:, units : 2 * units] = (hidden_grad * pre_up * slope).astype(jnp.bfloat16)
        hidden_out[:, 2 * units :] = (hidden_grad * activated).astype(jnp.bfloat16)

    def output_rows():
        return dot(kept[:, :units], down_here[...]) + dot(sent[:, :units], down_pair[...])

    def input_rows():
        total = None
        for gate_up, hidden in ((gate_up_here, kept), (gate_up_pair, sent)):
            for i in range(2):
                term = dot(hidden[:, (i + 1) * units : (i + 2) * units], gate_up[i])
                total = term if total is None else total + term
        return total

    def store(i, total):
        for m, merge in enumerate(merges):
            for j in range(groups):
                out = outs[(i * len(merges) + m) * groups + j]
                at = 0
                for u in merge:
                    low, high = bounds[u * groups + j], bounds[u * groups + j + 1]
                    out[at : at + high - low] = total[low:high].astype(out.dtype)
                    at += high - low

    for i, (kind, _) in enumerate(lanes):
        if kind == "up":
            store(i, output_rows())
        elif kind == "down":
            store(i, input_rows())
        else:

            @pl.when(section == 0)
            def _():
                store(i, output_rows())

            @pl.when(section != 0)
            def _():
                store(i, input_rows())


def weights_body(which, columns, hidden_refs, piece_refs, bundles, out, hidden_all, piece_all):
    units, width = out.shape[1:]
    at = 0
    for ref in hidden_refs:
        hidden_all[at : at + ref.shape[0]] = ref[...]
        at += ref.shape[0]
    at = 0
    for ref in piece_refs:
        piece_all[at : at + ref.shape[1]] = ref[which]
        at += ref.shape[1]
    for ref in bundles:
        piece_all[at : at + ref.shape[0]] = ref[:, which * width : (which + 1) * width]
        hidden_all[at : at + ref.shape[0]] = ref[:, 2 * width :]
        at += ref.shape[0]
    for i, c in enumerate(columns):
        value = dot(hidden_all[:, c * units : (c + 1) * units], piece_all[...], FIRST)
        out[i] = value.astype(out.dtype)


def final_body(mode, returns, blocks, where_ref, info, *refs):
    section = where_ref[0]
    count = len(returns)
    slots = [refs[r] for r in sorted(range(count), key=lambda r: returns[r])]
    outs, (value, zero, sems) = refs[count : count + len(mode)], refs[count + len(mode) :]
    rows_here, width = value.shape
    step = width // blocks
    place, scale = info[0:1], info[1:2]
    pick = jnp.where(
        lax.broadcasted_iota(jnp.int32, (rows_here, rows_here), 0).astype(jnp.float32) == place, 1.0, 0.0
    ).astype(jnp.bfloat16)
    scale_column = column_of(scale)

    def write(target, others):
        copies = []
        if others:
            zero[...] = jnp.zeros_like(zero)
        for i, other in enumerate(others):
            copies.append(pltpu.make_async_copy(zero, other, sems.at[blocks + i]))
            copies[-1].start()
        for b in range(blocks):
            at = slice(b * step, (b + 1) * step)
            rows = jnp.concatenate([ref[:, at] for ref in slots])
            value[:, at] = (dot(pick, rows, FIRST) * scale_column).astype(jnp.bfloat16)
            if target is not None:
                here = pl.ds(b * step, step)
                copies.append(pltpu.make_async_copy(value.at[:, here], target.at[:, here], sems.at[b]))
                copies[-1].start()
        for copy in copies:
            copy.wait()

    for i, (lowest, highest) in enumerate(mode):

        @pl.when((section >= lowest) & (section <= highest))
        def _(i=i):
            write(outs[i], [out for n, out in enumerate(outs) if n != i])

    if len(mode) == 1:

        @pl.when((section < mode[0][0]) | (section > mode[0][1]))
        def _():
            write(None, list(outs))


def plan(window, capacity):
    if window < 4:
        units = [(k, 0, capacity) for k in range(window)]
        return units, [[[k] for k in range(window)]]
    half = capacity // 2
    units = [(k, 0, capacity) for k in range(2)]
    for k in range(2, window):
        units += [(k, 0, half), (k, half, capacity)]
    pairs = [[[u, u + 1]] for u in range(2, len(units), 2)]
    return units, [[[0]], [[1]]] + pairs


def computed(tokens, cotangent, routes, gates, gate_up, down):
    sections, copies, window = (lax.axis_size(axis) for axis in AXES)
    groups = copies // 2
    rows_here, width = tokens.shape[1:]
    capacity = rows_here // window
    position = jnp.stack([lax.axis_index("section"), lax.axis_index("expert")]).astype(jnp.int32)

    def pair_of(s, d, e):
        return s, d ^ 1, e

    def group_shift(step):
        return lambda s, d, e: (s, (d // 2 + step) % groups * 2 + d % 2, e)

    def column_shift(step):
        return lambda s, d, e: (s, d, (e + step) % window)

    def owner_shift(up, step):
        def target(s, d, e):
            to = (s + up) % sections if sections == 2 else s + up
            return (to, d, (e + step) % window) if 0 <= to < sections else None

        return target

    lanes = (("swap", 1),) if sections == 2 else (("up", 1), ("down", -1))
    bf16 = functools.partial(jax.ShapeDtypeStruct, dtype=jnp.bfloat16)
    f32 = functools.partial(jax.ShapeDtypeStruct, dtype=jnp.float32)

    units, chunks = plan(window, capacity)
    step = width // 4 if width % 512 == 0 else width
    *packed, info = pl.pallas_call(
        functools.partial(pack_body, window, units, lanes),
        out_shape=[bf16((2, high - low, width)) for _, low, high in units] + [f32((len(lanes), 2, rows_here))],
        in_specs=[IN_SMEM] + [IN_HBM] * 4,
        out_specs=[IN_VMEM] * (len(units) + 1),
        scratch_shapes=[pltpu.VMEM((rows_here, width), jnp.bfloat16)] * 2
        + [pltpu.VMEM((routes.shape[2], 1, rows_here), dtype) for dtype in (routes.dtype, gates.dtype)]
        + [pltpu.SemaphoreType.DMA((2, width // step)), pltpu.SemaphoreType.DMA((2,))],
        compiler_params=pltpu.CompilerParams(vmem_limit_bytes=12 << 20),
        name="pack",
    )(
        position,
        in_hbm(jnp.transpose(routes, (2, 0, 1))),
        in_hbm(jnp.transpose(gates, (2, 0, 1))),
        in_hbm(tokens[0]),
        in_hbm(cotangent[0]),
    )
    infos = [moved(info[i], owner_shift(up, 0)) for i, (_, up) in enumerate(lanes)]

    gate_up_here, down_here = gate_up[0, 0], down[0, 0]
    gate_up_pair = moved(gate_up_here, pair_of)
    down_pair = moved(down_here, pair_of)
    hidden_units = down_here.shape[0]
    gate_up_here, down_here = pl.pallas_call(
        functools.partial(fetch_body, 2),
        out_shape=[bf16(gate_up_here.shape), bf16(down_here.shape)],
        in_specs=[IN_HBM] * 2,
        out_specs=[IN_VMEM] * 2,
        scratch_shapes=[pltpu.SemaphoreType.DMA((3, 2))],
        compiler_params=pltpu.CompilerParams(vmem_limit_bytes=12 << 20),
        name="fetch",
    )(in_hbm(gate_up_here), in_hbm(down_here))
    weights = (gate_up_here, down_here, gate_up_pair, down_pair)
    weights = tuple(pltpu.with_memory_space_constraint(w, pltpu.VMEM) for w in weights)

    arrived = [moved(packed[u], column_shift(k)) if k else packed[u] for u, (k, _, _) in enumerate(units)]
    returned = [[] for _ in lanes]
    returns = []
    kept_pieces, kept_hidden, bundles = [], [], []
    for chunk in chunks:
        pieces, part_shapes, merges = [], [], []
        for merge in chunk:
            merges.append([len(pieces) // groups + m for m in range(len(merge))])
            for u in merge:
                pieces += [moved(arrived[u], group_shift(j)) if j else arrived[u] for j in range(groups)]
            size = (sum(units[u][2] - units[u][1] for u in merge), width)
            part_shapes += [f32(size)] + [bf16(size)] * (groups - 1)
            returns.append(units[merge[0]])
        chunk_rows = sum(piece.shape[1] for piece in pieces)
        *parts, kept, bundle = call(
            functools.partial(chunk_body, lanes, groups, merges),
            part_shapes * len(lanes)
            + [bf16((chunk_rows, 3 * hidden_units)), bf16((chunk_rows, 2 * width + 3 * hidden_units))],
            (position, *pieces, *weights),
            16,
        )
        kept_pieces += pieces
        kept_hidden.append(kept)
        bundles.append(moved(bundle, pair_of))
        for i, (_, up) in enumerate(lanes):
            for m, merge in enumerate(chunk):
                at = (i * len(chunk) + m) * groups
                total = parts[at]
                for j in range(1, groups):
                    back = moved(parts[at + j], group_shift(-j))
                    total = total + back.astype(jnp.float32)
                returned[i].append(moved(total.astype(jnp.bfloat16), owner_shift(up, -units[merge[0]][0])))

    def weights_call(which, columns):
        operands = (*kept_hidden, *kept_pieces, *bundles)
        n, m = len(kept_hidden), len(kept_hidden) + len(kept_pieces)

        def body(*refs):
            at = len(operands)
            weights_body(which, columns, refs[:n], refs[n:m], refs[m:at], *refs[at:])

        contracted = 2 * sum(piece.shape[1] for piece in kept_pieces)
        return call(
            body,
            [bf16((len(columns), hidden_units, width))],
            operands,
            16,
            [
                pltpu.VMEM((contracted, 3 * hidden_units), jnp.bfloat16),
                pltpu.VMEM((contracted, width), jnp.bfloat16),
            ],
            smem=0,
        )[0]

    grad_down = weights_call(1, (0,))
    grad_gate_up = weights_call(0, (1, 2))

    modes = {
        "swap": ((1, 1), (0, 0)),
        "up": ((1, sections - 1),),
        "down": ((0, sections - 2),),
    }
    results = []
    for i, (kind, _) in enumerate(lanes):
        count = len(modes[kind])
        blocks = width // step
        results += pl.pallas_call(
            functools.partial(final_body, modes[kind], returns, blocks),
            out_shape=[bf16((rows_here, width))] * count,
            in_specs=[IN_SMEM] + [IN_VMEM] * (1 + len(returns)),
            out_specs=[IN_HBM] * count,
            scratch_shapes=[pltpu.VMEM((rows_here, width), jnp.bfloat16)] * 2
            + [pltpu.SemaphoreType.DMA((blocks + count,))],
            compiler_params=pltpu.CompilerParams(vmem_limit_bytes=12 << 20),
            name="final",
        )(position, infos[i], *returned[i])
    return (results[0][None], results[1][None], grad_gate_up[None, None], grad_down[None])


def solution(mesh):
    tokens_spec = P("section", ("dp", "expert"), None)
    gate_up_spec = P("section", "expert", None, "dp", None)
    down_spec = P("section", "expert", "dp", None)
    return jax.shard_map(
        computed,
        mesh=mesh,
        in_specs=(tokens_spec,) * 4 + (gate_up_spec, down_spec),
        out_specs=(tokens_spec, tokens_spec, gate_up_spec, down_spec),
        check_vma=False,
    )
```

```python
import functools

import jax
import jax.numpy as jnp
from jax import lax
from jax.experimental import pallas as pl
from jax.experimental.pallas import tpu as pltpu
from jax.sharding import PartitionSpec as P


AXES = ("section", "dp", "expert")
LAST = (((1,), (1,)), ((), ()))
FIRST = (((0,), (0,)), ((), ()))
PLAIN = (((1,), (0,)), ((), ()))
IN_VMEM = pl.BlockSpec(memory_space=pltpu.VMEM)
IN_HBM = pl.BlockSpec(memory_space=pltpu.HBM)
IN_SMEM = pl.BlockSpec(memory_space=pltpu.SMEM)


def moved(value, target):
    sizes = [lax.axis_size(axis) for axis in AXES]
    pairs = []
    for s in range(sizes[0]):
        for d in range(sizes[1]):
            for e in range(sizes[2]):
                to = target(s, d, e)
                if to is not None:
                    source = (s * sizes[1] + d) * sizes[2] + e
                    pairs.append((source, (to[0] * sizes[1] + to[1]) * sizes[2] + to[2]))
    return lax.ppermute(value, AXES, pairs)


def in_hbm(value):
    return pltpu.with_memory_space_constraint(value, pltpu.HBM)


def dot(a, b, dims=PLAIN):
    return lax.dot_general(a, b, dims, preferred_element_type=jnp.float32)


def call(body, outs, operands, mib, scratch=(), smem=1):
    return pl.pallas_call(
        body,
        out_shape=outs,
        in_specs=[IN_SMEM] * smem + [IN_VMEM] * (len(operands) - smem),
        out_specs=[IN_VMEM] * len(outs),
        scratch_shapes=scratch,
        compiler_params=pltpu.CompilerParams(vmem_limit_bytes=mib << 20),
    )(*operands)


def column_of(row):
    n = row.shape[1]
    diagonal = lax.broadcasted_iota(jnp.int32, (n, n), 0) == lax.broadcasted_iota(jnp.int32, (n, n), 1)
    return jnp.sum(jnp.where(diagonal, row, 0.0), 1, keepdims=True)


def pack_body(window, units, lanes, where_ref, routes, gates, tokens, cotangent, *refs):
    section, column = where_ref[0], where_ref[1]
    packed, info, refs = refs[: len(units)], refs[len(units)], refs[len(units) + 1 :]
    tokens_here, cotangent_here, routes_here, gates_here, sems, small_sems = refs
    rows_here = tokens.shape[0]
    capacity = rows_here // window
    small = [
        pltpu.make_async_copy(far, near, small_sems.at[which])
        for which, (far, near) in enumerate(((routes, routes_here), (gates, gates_here)))
    ]
    large = [
        pltpu.make_async_copy(far, near, sems.at[which])
        for which, (far, near) in enumerate(((tokens, tokens_here), (cotangent, cotangent_here)))
    ]
    for copy in small + large:
        copy.start()
    for copy in small:
        copy.wait()
    expert_of = jnp.full((1, rows_here), -1, jnp.int32)
    weight = jnp.zeros((1, rows_here), jnp.float32)
    for i in range(routes.shape[0]):
        in_window = routes_here[i] < window
        expert_of = jnp.where(in_window, routes_here[i], expert_of)
        weight = jnp.where(in_window, gates_here[i], weight)
    present = expert_of >= 0
    distance = expert_of - column
    distance = jnp.where(distance < 0, distance + window, distance)
    code = jnp.where(present, distance, -1).astype(jnp.float32)
    square = (rows_here, rows_here)
    down_index = lax.broadcasted_iota(jnp.int32, square, 0)
    along_index = lax.broadcasted_iota(jnp.int32, square, 1)
    earlier = (column_of(code) == code) & (down_index < along_index)
    slot = jnp.sum(jnp.where(earlier, 1.0, 0.0), 0, keepdims=True)
    place = jnp.where(present, code * capacity + slot, -1.0)
    select = jnp.where(down_index.astype(jnp.float32) == place, 1.0, 0.0).astype(jnp.bfloat16)
    for i, (kind, _) in enumerate(lanes):
        ones = jnp.ones_like(weight)
        scale = {"up": weight, "down": ones, "swap": jnp.where(section == 0, weight, ones)}[kind]
        info[i, 0:1] = place
        info[i, 1:2] = scale
    scale_column = column_of(weight)
    for which in range(2):
        large[which].wait()
        if which:
            block = (cotangent_here[...].astype(jnp.float32) * scale_column).astype(jnp.bfloat16)
        else:
            block = tokens_here[...]
        slots = dot(select, block).astype(jnp.bfloat16)
        for out, (k, low, high) in zip(packed, units):
            out[which] = slots[k * capacity + low : k * capacity + high]


def fetch_body(blocks, gate_up, down, gate_up_out, down_out, sems):
    copies = []
    for which, (far, near) in enumerate(((gate_up.at[0], gate_up_out.at[0]), (gate_up.at[1], gate_up_out.at[1]), (down, down_out))):
        step = far.shape[0] // blocks
        for b in range(blocks):
            at = pl.ds(b * step, step)
            copies.append(pltpu.make_async_copy(far.at[at], near.at[at], sems.at[which, b]))
            copies[-1].start()
    for copy in copies:
        copy.wait()


def chunk_body(lanes, groups, merges, where_ref, *refs):
    section = where_ref[0]
    count = groups * sum(len(merge) for merge in merges)
    pieces, refs = refs[:count], refs[count:]
    (gate_up_here, down_here, gate_up_pair, down_pair), refs = refs[:4], refs[4:]
    outs, (kept, bundle) = refs[:-2], refs[-2:]
    units, width = down_here.shape
    bounds = [0]
    for piece in pieces:
        bounds.append(bounds[-1] + piece.shape[1])
        at = slice(bounds[-2], bounds[-1])
        bundle[at, :width] = piece[0]
        bundle[at, width : 2 * width] = piece[1]
    rows, grads = bundle[:, :width], bundle[:, width : 2 * width]
    sent = bundle.at[:, 2 * width :]
    for gate_up, down, hidden_out in ((gate_up_here, down_here, kept), (gate_up_pair, down_pair, sent)):
        pre_gate = dot(gate_up[0], rows, LAST).T
        pre_up = dot(gate_up[1], rows, LAST).T
        hidden_grad = dot(down[...], grads, LAST).T
        sigmoid = jax.nn.sigmoid(pre_gate)
        activated = pre_gate * sigmoid
        slope = sigmoid * (1.0 + pre_gate * (1.0 - sigmoid))
        hidden_out[:, :units] = (activated * pre_up).astype(jnp.bfloat16)
        hidden_out[:, units : 2 * units] = (hidden_grad * pre_up * slope).astype(jnp.bfloat16)
        hidden_out[:, 2 * units :] = (hidden_grad * activated).astype(jnp.bfloat16)

    def output_rows():
        return dot(kept[:, :units], down_here[...]) + dot(sent[:, :units], down_pair[...])

    def input_rows():
        total = None
        for gate_up, hidden in ((gate_up_here, kept), (gate_up_pair, sent)):
            for i in range(2):
                term = dot(hidden[:, (i + 1) * units : (i + 2) * units], gate_up[i])
                total = term if total is None else total + term
        return total

    def store(i, total):
        for m, merge in enumerate(merges):
            for j in range(groups):
                out = outs[(i * len(merges) + m) * groups + j]
                at = 0
                for u in merge:
                    low, high = bounds[u * groups + j], bounds[u * groups + j + 1]
                    out[at : at + high - low] = total[low:high].astype(out.dtype)
                    at += high - low

    for i, (kind, _) in enumerate(lanes):
        if kind == "up":
            store(i, output_rows())
        elif kind == "down":
            store(i, input_rows())
        else:

            @pl.when(section == 0)
            def _():
                store(i, output_rows())

            @pl.when(section != 0)
            def _():
                store(i, input_rows())


def weights_body(which, columns, hidden_refs, piece_refs, bundles, out, hidden_all, piece_all):
    units, width = out.shape[1:]
    at = 0
    for ref in hidden_refs:
        hidden_all[at : at + ref.shape[0]] = ref[...]
        at += ref.shape[0]
    at = 0
    for ref in piece_refs:
        piece_all[at : at + ref.shape[1]] = ref[which]
        at += ref.shape[1]
    for ref in bundles:
        piece_all[at : at + ref.shape[0]] = ref[:, which * width : (which + 1) * width]
        hidden_all[at : at + ref.shape[0]] = ref[:, 2 * width :]
        at += ref.shape[0]
    for i, c in enumerate(columns):
        value = dot(hidden_all[:, c * units : (c + 1) * units], piece_all[...], FIRST)
        out[i] = value.astype(out.dtype)


def final_body(mode, returns, blocks, where_ref, info, *refs):
    section = where_ref[0]
    count = len(returns)
    slots = [refs[r] for r in sorted(range(count), key=lambda r: returns[r])]
    outs, (value, zero, sems) = refs[count : count + len(mode)], refs[count + len(mode) :]
    rows_here, width = value.shape
    step = width // blocks
    place, scale = info[0:1], info[1:2]
    pick = jnp.where(
        lax.broadcasted_iota(jnp.int32, (rows_here, rows_here), 0).astype(jnp.float32) == place, 1.0, 0.0
    ).astype(jnp.bfloat16)
    scale_column = column_of(scale)

    def write(target, others):
        copies = []
        if others:
            zero[...] = jnp.zeros_like(zero)
        for i, other in enumerate(others):
            copies.append(pltpu.make_async_copy(zero, other, sems.at[blocks + i]))
            copies[-1].start()
        for b in range(blocks):
            at = slice(b * step, (b + 1) * step)
            rows = jnp.concatenate([ref[:, at] for ref in slots])
            value[:, at] = (dot(pick, rows, FIRST) * scale_column).astype(jnp.bfloat16)
            if target is not None:
                here = pl.ds(b * step, step)
                copies.append(pltpu.make_async_copy(value.at[:, here], target.at[:, here], sems.at[b]))
                copies[-1].start()
        for copy in copies:
            copy.wait()

    for i, (lowest, highest) in enumerate(mode):

        @pl.when((section >= lowest) & (section <= highest))
        def _(i=i):
            write(outs[i], [out for n, out in enumerate(outs) if n != i])

    if len(mode) == 1:

        @pl.when((section < mode[0][0]) | (section > mode[0][1]))
        def _():
            write(None, list(outs))


def plan(window, capacity):
    if window < 4:
        units = [(k, 0, capacity) for k in range(window)]
        return units, [[[k] for k in range(window)]]
    half = capacity // 2
    units = [(k, 0, capacity) for k in range(2)]
    for k in range(2, window):
        units += [(k, 0, half), (k, half, capacity)]
    pairs = [[[u, u + 1]] for u in range(2, len(units), 2)]
    return units, [[[0]], [[1]]] + pairs


def computed(tokens, cotangent, routes, gates, gate_up, down):
    sections, copies, window = (lax.axis_size(axis) for axis in AXES)
    groups = copies // 2
    rows_here, width = tokens.shape[1:]
    capacity = rows_here // window
    position = jnp.stack([lax.axis_index("section"), lax.axis_index("expert")]).astype(jnp.int32)

    def pair_of(s, d, e):
        return s, d ^ 1, e

    def group_shift(step):
        return lambda s, d, e: (s, (d // 2 + step) % groups * 2 + d % 2, e)

    def column_shift(step):
        return lambda s, d, e: (s, d, (e + step) % window)

    def owner_shift(up, step):
        def target(s, d, e):
            to = (s + up) % sections if sections == 2 else s + up
            return (to, d, (e + step) % window) if 0 <= to < sections else None

        return target

    lanes = (("swap", 1),) if sections == 2 else (("up", 1), ("down", -1))
    bf16 = functools.partial(jax.ShapeDtypeStruct, dtype=jnp.bfloat16)
    f32 = functools.partial(jax.ShapeDtypeStruct, dtype=jnp.float32)

    units, chunks = plan(window, capacity)
    *packed, info = pl.pallas_call(
        functools.partial(pack_body, window, units, lanes),
        out_shape=[bf16((2, high - low, width)) for _, low, high in units] + [f32((len(lanes), 2, rows_here))],
        in_specs=[IN_SMEM] + [IN_HBM] * 4,
        out_specs=[IN_VMEM] * (len(units) + 1),
        scratch_shapes=[pltpu.VMEM((rows_here, width), jnp.bfloat16)] * 2
        + [pltpu.VMEM((routes.shape[2], 1, rows_here), dtype) for dtype in (routes.dtype, gates.dtype)]
        + [pltpu.SemaphoreType.DMA((2,)), pltpu.SemaphoreType.DMA((2,))],
        compiler_params=pltpu.CompilerParams(vmem_limit_bytes=12 << 20),
        name="pack",
    )(
        position,
        in_hbm(jnp.transpose(routes, (2, 0, 1))),
        in_hbm(jnp.transpose(gates, (2, 0, 1))),
        in_hbm(tokens[0]),
        in_hbm(cotangent[0]),
    )
    infos = [moved(info[i], owner_shift(up, 0)) for i, (_, up) in enumerate(lanes)]

    gate_up_here, down_here = gate_up[0, 0], down[0, 0]
    gate_up_pair = moved(gate_up_here, pair_of)
    down_pair = moved(down_here, pair_of)
    hidden_units = down_here.shape[0]
    gate_up_here, down_here = pl.pallas_call(
        functools.partial(fetch_body, 2),
        out_shape=[bf16(gate_up_here.shape), bf16(down_here.shape)],
        in_specs=[IN_HBM] * 2,
        out_specs=[IN_VMEM] * 2,
        scratch_shapes=[pltpu.SemaphoreType.DMA((3, 2))],
        compiler_params=pltpu.CompilerParams(vmem_limit_bytes=12 << 20),
        name="fetch",
    )(in_hbm(gate_up_here), in_hbm(down_here))
    weights = (gate_up_here, down_here, gate_up_pair, down_pair)
    weights = tuple(pltpu.with_memory_space_constraint(w, pltpu.VMEM) for w in weights)

    arrived = [moved(packed[u], column_shift(k)) if k else packed[u] for u, (k, _, _) in enumerate(units)]
    returned = [[] for _ in lanes]
    returns = []
    kept_pieces, kept_hidden, bundles = [], [], []
    for chunk in chunks:
        pieces, part_shapes, merges = [], [], []
        for merge in chunk:
            merges.append([len(pieces) // groups + m for m in range(len(merge))])
            for u in merge:
                pieces += [moved(arrived[u], group_shift(j)) if j else arrived[u] for j in range(groups)]
            size = (sum(units[u][2] - units[u][1] for u in merge), width)
            part_shapes += [f32(size)] + [bf16(size)] * (groups - 1)
            returns.append(units[merge[0]])
        chunk_rows = sum(piece.shape[1] for piece in pieces)
        *parts, kept, bundle = call(
            functools.partial(chunk_body, lanes, groups, merges),
            part_shapes * len(lanes)
            + [bf16((chunk_rows, 3 * hidden_units)), bf16((chunk_rows, 2 * width + 3 * hidden_units))],
            (position, *pieces, *weights),
            16,
        )
        kept_pieces += pieces
        kept_hidden.append(kept)
        bundles.append(moved(bundle, pair_of))
        for i, (_, up) in enumerate(lanes):
            for m, merge in enumerate(chunk):
                at = (i * len(chunk) + m) * groups
                total = parts[at]
                for j in range(1, groups):
                    back = moved(parts[at + j], group_shift(-j))
                    total = total + back.astype(jnp.float32)
                returned[i].append(moved(total.astype(jnp.bfloat16), owner_shift(up, -units[merge[0]][0])))

    def weights_call(which, columns):
        operands = (*kept_hidden, *kept_pieces, *bundles)
        n, m = len(kept_hidden), len(kept_hidden) + len(kept_pieces)

        def body(*refs):
            at = len(operands)
            weights_body(which, columns, refs[:n], refs[n:m], refs[m:at], *refs[at:])

        contracted = 2 * sum(piece.shape[1] for piece in kept_pieces)
        return call(
            body,
            [bf16((len(columns), hidden_units, width))],
            operands,
            16,
            [
                pltpu.VMEM((contracted, 3 * hidden_units), jnp.bfloat16),
                pltpu.VMEM((contracted, width), jnp.bfloat16),
            ],
            smem=0,
        )[0]

    grad_down = weights_call(1, (0,))
    grad_gate_up = weights_call(0, (1, 2))

    modes = {
        "swap": ((1, 1), (0, 0)),
        "up": ((1, sections - 1),),
        "down": ((0, sections - 2),),
    }
    results = []
    for i, (kind, _) in enumerate(lanes):
        count = len(modes[kind])
        blocks = 2
        results += pl.pallas_call(
            functools.partial(final_body, modes[kind], returns, blocks),
            out_shape=[bf16((rows_here, width))] * count,
            in_specs=[IN_SMEM] + [IN_VMEM] * (1 + len(returns)),
            out_specs=[IN_HBM] * count,
            scratch_shapes=[pltpu.VMEM((rows_here, width), jnp.bfloat16)] * 2
            + [pltpu.SemaphoreType.DMA((blocks + count,))],
            compiler_params=pltpu.CompilerParams(vmem_limit_bytes=12 << 20),
            name="final",
        )(position, infos[i], *returned[i])
    return (results[0][None], results[1][None], grad_gate_up[None, None], grad_down[None])


def solution(mesh):
    tokens_spec = P("section", ("dp", "expert"), None)
    gate_up_spec = P("section", "expert", None, "dp", None)
    down_spec = P("section", "expert", "dp", None)
    return jax.shard_map(
        computed,
        mesh=mesh,
        in_specs=(tokens_spec,) * 4 + (gate_up_spec, down_spec),
        out_specs=(tokens_spec, tokens_spec, gate_up_spec, down_spec),
        check_vma=False,
    )
```
